256 devices in a mesh: segment: 2 (over core), seq: 128 (over x, y, z).
Axes of the slice: x: 4, y: 4, z: 8, core: 2. Of those that a mesh axis runs over, the one named last changes fastest.
Arguments:
- activations: bfloat16 [2, 32768, 768], P('segment', 'seq'), may hold values from -6 to 6
- short_filters: bfloat16 [2, 128, 768], replicated, may hold values from -0.5 to 0.5
- long_filters: float32 [2, 32768, 768], P('segment', 'seq'), may hold values from -4 to 4
- skip_gain: float32 [2, 768], replicated, may hold values from -1 to 1
Outputs:
- sections: bfloat16 [2, 32768, 768], P('segment', 'seq')
The draws below stay inside these ranges and needn't reach their ends.
All inputs are finite; a program needn't handle non-finite values.
Results may differ from the reference program's by a relative error of at most 0.012.
Values may be sent and summed in bfloat16 or wider, within the bound.
A program may use at most 64 MiB of HBM per device.

```python
import math
import jax
import jax.numpy as jnp
from jax import lax

D = 768
COLS = 256
SHORT = 128
SECTIONS = 2
L = 32768
FFT_LEN = 65536
ROWS = 256


def draw_long_filters(key, part):
    rate_key = jax.random.fold_in(key, 11)
    noise_key = jax.random.fold_in(key, 23)
    rates = jnp.exp(jax.random.uniform(rate_key, (SECTIONS, 1, D), jnp.float32, math.log(0.25), math.log(64.0)))
    positions = jnp.arange(L, dtype=jnp.float32)[None, :, None] / L
    envelope = jnp.exp(-rates * positions)
    noise = jnp.clip(jax.random.normal(noise_key, (SECTIONS, L, D), jnp.float32), -4.0, 4.0)
    return noise * envelope


def block_scale(key, shape, cuts, low, top_value):
    def one(dim, shards_of):
        heights = jax.random.uniform(jax.random.fold_in(jax.random.fold_in(key, 6), dim), (shards_of,), jnp.float32, low / len(cuts), top_value / len(cuts))
        return jnp.repeat(jnp.exp(heights), shape[dim] // shards_of).reshape((-1,) + (1,) * (len(shape) - dim - 1))

    gain = one(*cuts[0])
    for cut in cuts[1:]:
        gain = gain * one(*cut)
    return gain


def bell_draw(stream_key, extent, width, bound, shards=(), held_as=jnp.bfloat16):
    gain = block_scale(stream_key, extent, shards, -0.22, 0.18) if shards else 1.0
    drawn = jax.random.normal(stream_key, extent, jnp.float32) * width * gain
    return jnp.minimum(jnp.maximum(drawn, -bound), bound).astype(held_as)


def setup_inputs(seed: int = 0) -> dict:
    splits = jax.random.split(jax.random.key(seed), 5)
    activations = bell_draw(splits[0], (SECTIONS, L, D), 1.0, 6.0, ((0, 2), (1, 128)))
    short_filters = bell_draw(splits[1], (SECTIONS, SHORT, D), SHORT ** -0.5, 0.5)
    long_filters = draw_long_filters(jax.random.fold_in(splits[4], 71), 0)
    skip_gain = jnp.clip(jax.random.uniform(splits[3], (SECTIONS, D), jnp.float32, -1.0, 1.0), -1.0, 1.0)
    return {"activations": activations, "short_filters": short_filters, "long_filters": long_filters, "skip_gain": skip_gain}


def row_table(grid_rows):
    real_rows = grid_rows // 2
    phases = (jnp.arange(grid_rows, dtype=jnp.int32)[:, None] * jnp.arange(real_rows, dtype=jnp.int32)[None, :] % grid_rows).astype(jnp.float32) * (2.0 * math.pi / grid_rows)
    return jnp.stack([jnp.cos(phases), -jnp.sin(phases)]).astype(jnp.bfloat16)

def back_row_table(grid_rows):
    real_rows = grid_rows // 2
    phases = (jnp.arange(real_rows, dtype=jnp.int32)[:, None] * jnp.arange(grid_rows, dtype=jnp.int32)[None, :] % grid_rows).astype(jnp.float32) * (2.0 * math.pi / grid_rows)
    return jnp.stack([jnp.cos(phases), -jnp.sin(phases)], axis=1).astype(jnp.bfloat16)

def column_table(width_cols, direction):
    phases = (jnp.arange(width_cols, dtype=jnp.int32)[:, None] * jnp.arange(width_cols, dtype=jnp.int32)[None, :] % width_cols).astype(jnp.float32) * (2.0 * math.pi / width_cols)
    cosine = jnp.cos(phases)
    sine_part = direction * jnp.sin(phases)
    return jnp.stack([jnp.stack([cosine, -sine_part], axis=1), jnp.stack([sine_part, cosine], axis=1)]).astype(jnp.bfloat16)

def twiddle(freq_index, col_index, fft_len):
    phases = (freq_index[:, None] * col_index[None, :] % fft_len).astype(jnp.float32) * (2.0 * math.pi / fft_len)
    return (jnp.cos(phases)[:, :, None], jnp.sin(phases)[:, :, None])

def complex_times(left, right):
    return jnp.stack([left[0] * right[0] - left[1] * right[1], left[0] * right[1] + left[1] * right[0]])

def short_conv(padded, tap_block):
    kernel = tap_block[::-1].astype(jnp.float32)[:, None, :]
    result = lax.conv_general_dilated(padded.astype(jnp.float32)[None], kernel, (1,), 'VALID', dimension_numbers=('NWC', 'WIO', 'NWC'), feature_group_count=tap_block.shape[1], precision=lax.Precision.HIGHEST)
    return result[0].astype(jnp.bfloat16)

def whole_forward(signal):
    token_grid = signal.reshape(ROWS // 2, COLS, signal.shape[1])
    first_pass = jnp.einsum('pka,abw->pkbw', row_table(ROWS).astype(jnp.float32), token_grid.astype(jnp.float32), precision=lax.Precision.HIGHEST)
    cosine, sine_part = twiddle(jnp.arange(ROWS, dtype=jnp.int32), jnp.arange(COLS, dtype=jnp.int32), FFT_LEN)
    turned = jnp.stack([first_pass[0] * cosine + first_pass[1] * sine_part, first_pass[1] * cosine - first_pass[0] * sine_part]).astype(jnp.bfloat16)
    return jnp.einsum('qdpb,pkbw->qkdw', column_table(COLS, -1.0).astype(jnp.float32), turned.astype(jnp.float32), precision=lax.Precision.HIGHEST)

def whole_inverse(product):
    back_cols = jnp.einsum('qdpb,pkbw->qkdw', column_table(COLS, 1.0).astype(jnp.float32), product.astype(jnp.float32), precision=lax.Precision.HIGHEST)
    cosine, sine_part = twiddle(jnp.arange(ROWS, dtype=jnp.int32), jnp.arange(COLS, dtype=jnp.int32), FFT_LEN)
    turned = jnp.stack([back_cols[0] * cosine - back_cols[1] * sine_part, back_cols[0] * sine_part + back_cols[1] * cosine]).astype(jnp.bfloat16)
    rows_out = jnp.einsum('apk,pkbw->abw', back_row_table(ROWS).astype(jnp.float32), turned.astype(jnp.float32), precision=lax.Precision.HIGHEST)
    scale = 1.0 / (FFT_LEN * math.sqrt(L))
    return (rows_out * scale).astype(jnp.bfloat16).reshape(L, product.shape[3])

def section_whole(signal, tap_block, filter_block, gain_block):
    padded = jnp.concatenate([jnp.zeros((SHORT - 1, signal.shape[1]), jnp.bfloat16), signal], axis=0)
    filtered_short = short_conv(padded, tap_block)
    spectrum = whole_forward(filter_block.astype(jnp.bfloat16))
    signal_spec = whole_forward(filtered_short)
    product = complex_times(signal_spec, spectrum).astype(jnp.bfloat16)
    filtered_long = whole_inverse(product)
    return (filtered_long.astype(jnp.float32) + gain_block[None, :] * filtered_short.astype(jnp.float32)).astype(jnp.bfloat16)

def reference(activations, short_filters, long_filters, skip_gain):
    block_width = math.gcd(D, 64)
    block_count = D // block_width

    def to_blocks(array):
        return jnp.moveaxis(array.reshape(array.shape[:-1] + (block_count, block_width)), -2, 0)

    def from_blocks(array):
        return jnp.moveaxis(array, 0, -2).reshape(array.shape[1:-1] + (D,))

    def run_whole(section_index, signal):

        def process(pieces):
            return section_whole(pieces[0], pieces[1], pieces[2], pieces[3])
        outputs = lax.map(process, (to_blocks(signal), to_blocks(short_filters[section_index]), to_blocks(long_filters[section_index]), to_blocks(skip_gain[section_index])))
        return from_blocks(outputs)
    first_out = run_whole(0, activations[0])
    gated = (first_out.astype(jnp.float32) * activations[1].astype(jnp.float32)).astype(jnp.bfloat16)
    second_out = run_whole(1, gated)
    return jnp.stack([first_out, second_out])
```

```python
import functools
import math

import jax
import jax.numpy as jnp
import numpy as np
from jax import lax
from jax.experimental import pallas as pl
from jax.experimental.pallas import tpu as pltpu
from jax.sharding import PartitionSpec as P

KP = 144


def tables(rows, cols, width):
    half = rows // 2
    k1 = np.arange(KP)
    live = (k1 <= half).astype(np.float64)
    a = np.arange(width)
    ph = 2.0 * np.pi * ((k1[:, None] * a[None, :]) % rows) / rows
    row_fwd = np.concatenate([np.cos(ph) * live[:, None], -np.sin(ph) * live[:, None]], 0)
    weight = live * np.where((k1 == 0) | (k1 == half), 1.0, 2.0)
    row_back = np.concatenate([(np.cos(ph) * weight[:, None]).T, (-np.sin(ph) * weight[:, None]).T], 1)
    b = np.arange(cols)
    pc = 2.0 * np.pi * ((b[:, None] * b[None, :]) % cols) / cols
    c, s = np.cos(pc), np.sin(pc)
    col_fwd = np.block([[c, -s], [s, c]])
    col_back = np.block([[c, s], [-s, c]])
    tw = 2.0 * np.pi * ((k1[:, None] * b[None, :]) % (rows * cols)) / (rows * cols)
    bf = lambda x: jnp.asarray(x, jnp.bfloat16)
    return (
        bf(row_fwd), bf(row_back), bf(col_fwd), bf(col_back),
        jnp.asarray(np.stack([np.cos(tw), np.sin(tw)]), jnp.float32),
    )


def dot(a, b):
    return jnp.dot(a, b, preferred_element_type=jnp.float32)


def filter_kernel(scale, x_ref, f_ref, taps_ref, gain_ref, rf_ref, rb_ref, cf_ref, cb_ref, tw_ref,
                  out_ref, pad_ref):
    channels = x_ref.shape[1]
    rows, cols = x_ref.shape[2], x_ref.shape[3]
    b_in = lax.broadcasted_iota(jnp.int32, (cols, cols), 0)
    b_out = lax.broadcasted_iota(jnp.int32, (cols, cols), 1)

    def spectrum(grid):
        first = dot(rf_ref[...], grid)
        re, im = first[:KP], first[KP:]
        cosine, sine = tw_ref[0], tw_ref[1]
        turned = jnp.concatenate(
            [re * cosine + im * sine, im * cosine - re * sine], 1
        ).astype(jnp.bfloat16)
        return dot(turned, cf_ref[...])

    def inverse(product):
        back = dot(product, cb_ref[...])
        re, im = back[:, :cols], back[:, cols:]
        cosine, sine = tw_ref[0], tw_ref[1]
        turned = jnp.concatenate(
            [re * cosine - im * sine, re * sine + im * cosine], 0
        ).astype(jnp.bfloat16)
        return dot(rb_ref[...], turned) * scale

    def short(grid, taps):
        circ = pltpu.roll(
            jnp.broadcast_to(taps, (cols, cols)), 0, 1, stride=1, stride_axis=0
        )
        now = jnp.where(b_out >= b_in, circ, 0.0).astype(jnp.bfloat16)
        before = jnp.where(b_out < b_in, circ, 0.0).astype(jnp.bfloat16)
        pad_ref[8:, :] = grid.astype(jnp.float32)
        earlier = pad_ref[7:7 + rows, :].astype(jnp.bfloat16)
        return (dot(grid, now) + dot(earlier, before)).astype(jnp.bfloat16)

    pad_ref[...] = jnp.zeros_like(pad_ref)
    for c in range(channels):
        previous = None
        for s in range(2):
            grid = x_ref[s, c]
            if s:
                grid = (previous.astype(jnp.float32) * grid.astype(jnp.float32)).astype(jnp.bfloat16)
            z = short(grid, taps_ref[s * channels + c][None, :])
            signal = spectrum(z)
            kernel_spec = spectrum(f_ref[s, c])
            ar, ai = signal[:, :cols], signal[:, cols:]
            hr, hi = kernel_spec[:, :cols], kernel_spec[:, cols:]
            product = jnp.concatenate([ar * hr - ai * hi, ar * hi + ai * hr], 1).astype(jnp.bfloat16)
            long = inverse(product).astype(jnp.bfloat16).astype(jnp.float32)
            previous = (long + gain_ref[s, c] * z.astype(jnp.float32)).astype(jnp.bfloat16)
            out_ref[s, c] = previous


def body(activations, short_filters, long_filters, skip_gain):
    tokens, width = activations.shape[1:]
    segs, seqs = lax.axis_size("segment"), lax.axis_size("seq")
    parts = segs * seqs
    mine = width // parts
    cols, rows = tokens, 2 * seqs
    both = ("seq", "segment")
    first = (lax.axis_index("seq") * segs + lax.axis_index("segment")) * mine
    taps = lax.dynamic_slice_in_dim(short_filters, first, mine, 2)
    taps = jnp.swapaxes(taps, 1, 2).reshape(2 * mine, -1).astype(jnp.float32)
    taps = jnp.pad(taps, ((0, 0), (0, cols - taps.shape[1])))
    gains = lax.dynamic_slice_in_dim(skip_gain, first, mine, 1)

    def outward(block):
        turned = block.T.reshape(parts, mine, tokens)
        got = lax.all_to_all(turned, both, 0, 0, tiled=True)
        return got.reshape(seqs, segs, mine, tokens).transpose(1, 2, 0, 3)

    x = outward(activations[0])
    f = outward(long_filters[0].astype(jnp.bfloat16))
    scale = 1.0 / (rows * cols * math.sqrt(rows * cols // 2))
    vm = pl.BlockSpec(memory_space=pltpu.VMEM)
    sm = pl.BlockSpec(memory_space=pltpu.SMEM)
    out = pl.pallas_call(
        functools.partial(filter_kernel, scale),
        out_shape=jax.ShapeDtypeStruct((2, mine, seqs, tokens), jnp.bfloat16),
        in_specs=[vm, vm, vm, sm, vm, vm, vm, vm, vm],
        out_specs=vm,
        scratch_shapes=[pltpu.VMEM((seqs + 8, cols), jnp.float32)],
        compiler_params=pltpu.CompilerParams(vmem_limit_bytes=56 * 1024 * 1024),
    )(x, f, taps, gains, *tables(rows, cols, seqs))
    home = out.transpose(2, 0, 1, 3).reshape(parts, mine, tokens)
    back = lax.all_to_all(home, both, 0, 0, tiled=True)
    return back.reshape(width, tokens).T[None]


def solution(mesh):
    return jax.shard_map(
        body,
        mesh=mesh,
        in_specs=(P("segment", "seq", None), P(), P("segment", "seq", None), P()),
        out_specs=P("segment", "seq", None),
        check_vma=False,
    )
```

```python
import functools
import math

import jax
import jax.numpy as jnp
import numpy as np
from jax import lax
from jax.experimental import pallas as pl
from jax.experimental.pallas import tpu as pltpu
from jax.sharding import PartitionSpec as P

MESH = pl.DeviceIdType.MESH
COLS = 128


def tables(rows, cols):
    half = rows // 2
    kept = (half + 1 + 15) // 16 * 16
    k1 = np.arange(kept)
    live = (k1 <= half).astype(np.float64)
    a = np.arange(half)
    ph = 2.0 * np.pi * ((k1[:, None] * a[None, :]) % rows) / rows
    row_fwd = np.concatenate([np.cos(ph) * live[:, None], -np.sin(ph) * live[:, None]], 0)
    weight = live * np.where((k1 == 0) | (k1 == half), 1.0, 2.0)
    row_back = np.concatenate([(np.cos(ph) * weight[:, None]).T, (-np.sin(ph) * weight[:, None]).T], 1)
    b = np.arange(cols)
    pc = 2.0 * np.pi * ((b[:, None] * b[None, :]) % cols) / cols
    c, s = np.cos(pc), np.sin(pc)
    col_fwd = np.block([[c, -s], [s, c]])
    col_back = np.block([[c, s], [-s, c]])
    tw = 2.0 * np.pi * ((k1[:, None] * b[None, :]) % (rows * cols)) / (rows * cols)
    bf = lambda x: jnp.asarray(x, jnp.bfloat16)
    return (
        bf(row_fwd), bf(row_back), bf(col_fwd), bf(col_back),
        jnp.asarray(np.stack([np.cos(tw), np.sin(tw)]), jnp.float32),
    )


def dot(a, b):
    return jnp.dot(a, b, preferred_element_type=jnp.float32)


def kernel(scale, kept, x_ref, f_ref, taps_ref, gain_ref, rf_ref, rb_ref, cf_ref, cb_ref, tw_ref,
           out_ref, x_in, f_in, y_out, y_in, spec, send_sem, f_sem, x_sem, y_sem):
    channels = taps_ref.shape[0] // 2
    seqs = x_in.shape[2]
    rows, cols = 2 * seqs, x_in.shape[4]
    q, s = lax.axis_index("seq"), lax.axis_index("segment")
    zs = [lax.rem(q + d, 8) for d in range(8)]
    cores = [s, 1 - s]
    mine = q * 2 + s

    def everyone(copy_to, some_cores):
        def group(xy, is_first):
            for dz in range(8):
                for core in some_cores:
                    seq, core_now = xy + zs[dz], cores[core]
                    if not (is_first and dz == 0 and core == 0):
                        copy_to(seq, core_now)

        x, y = q // 32, lax.rem(q // 8, 4)
        group(q - zs[0], True)

        def step(g, carry):
            group(lax.rem(x + g // 4, 4) * 32 + lax.rem(y + lax.rem(g, 4), 4) * 8, False)
            return carry

        lax.fori_loop(1, 16, step, 0)

    def send_in(from_ref, to_ref, sent_sem, sem):
        pltpu.make_async_copy(from_ref.at[mine], to_ref.at[s, :, q], sem).start()
        everyone(
            lambda seq, core: pltpu.make_async_remote_copy(
                from_ref.at[seq * 2 + core], to_ref.at[s, :, q], sent_sem, sem,
                device_id={"segment": core, "seq": seq}, device_id_type=MESH,
            ).start(),
            (0, 1),
        )

    def send_out(section):
        def go(seq, core):
            pltpu.make_async_remote_copy(
                y_out.at[section, :, seq], y_in.at[mine], send_sem.at[2], y_sem,
                device_id={"segment": section, "seq": seq}, device_id_type=MESH,
            ).start()

        @pl.when(s == section)
        def _():
            pltpu.make_async_copy(y_out.at[section, :, q], y_in.at[mine], y_sem).start()
            everyone(go, (0,))

        @pl.when(s != section)
        def _():
            everyone(go, (1,))

    send_in(f_ref, f_in, send_sem.at[0], f_sem)
    send_in(x_ref, x_in, send_sem.at[1], x_sem)

    b_in = lax.broadcasted_iota(jnp.int32, (cols, cols), 0)
    b_out = lax.broadcasted_iota(jnp.int32, (cols, cols), 1)
    top = lax.broadcasted_iota(jnp.int32, (rows, cols), 0) == 0

    def spectrum(grids):
        first = dot(rf_ref[...], jnp.concatenate(grids, 1))
        turned = []
        for c in range(len(grids)):
            re, im = first[:kept, c * cols:(c + 1) * cols], first[kept:, c * cols:(c + 1) * cols]
            cosine, sine = tw_ref[0], tw_ref[1]
            turned.append(jnp.concatenate(
                [re * cosine + im * sine, im * cosine - re * sine], 1
            ).astype(jnp.bfloat16))
        return [dot(t, cf_ref[...]) for t in turned]

    def inverse(products):
        turned = []
        for product in products:
            back = dot(product, cb_ref[...])
            re, im = back[:, :cols], back[:, cols:]
            cosine, sine = tw_ref[0], tw_ref[1]
            turned.append(jnp.concatenate(
                [re * cosine - im * sine, re * sine + im * cosine], 0
            ).astype(jnp.bfloat16))
        y = dot(rb_ref[...], jnp.concatenate(turned, 1)) * scale
        return [y[:, c * cols:(c + 1) * cols] for c in range(len(products))]

    def short(grid, taps):
        circ = pltpu.roll(jnp.broadcast_to(taps, (cols, cols)), 0, 1, stride=1, stride_axis=0)
        both = jnp.concatenate(
            [jnp.where(b_out >= b_in, circ, 0.0), jnp.where(b_out < b_in, circ, 0.0)], 0
        ).astype(jnp.bfloat16)
        earlier = jnp.where(top, 0.0, pltpu.roll(grid, 1, 0))
        return dot(jnp.concatenate([grid, earlier], 1).astype(jnp.bfloat16), both).astype(jnp.bfloat16)

    pltpu.make_async_copy(f_in, f_in, f_sem).wait()
    for section in range(2):
        got = spectrum([f_in[section, c].reshape(rows, cols) for c in range(channels)])
        for c in range(channels):
            spec[section, c] = got[c]

    pltpu.make_async_copy(x_in, x_in, x_sem).wait()
    previous = None
    for section in range(2):
        zs_now = []
        for c in range(channels):
            grid = x_in[section, c].reshape(rows, cols).astype(jnp.float32)
            if section:
                grid = (previous[c] * grid).astype(jnp.bfloat16).astype(jnp.float32)
            zs_now.append(short(grid, taps_ref[section * channels + c][None, :]))
        products = []
        for c, signal in enumerate(spectrum(zs_now)):
            other = spec[section, c]
            ar, ai = signal[:, :cols], signal[:, cols:]
            hr, hi = other[:, :cols], other[:, cols:]
            products.append(
                jnp.concatenate([ar * hr - ai * hi, ar * hi + ai * hr], 1).astype(jnp.bfloat16)
            )
        previous = []
        for c, long in enumerate(inverse(products)):
            y = (
                long.astype(jnp.bfloat16).astype(jnp.float32)
                + gain_ref[section, c] * zs_now[c].astype(jnp.float32)
            ).astype(jnp.bfloat16)
            previous.append(y.astype(jnp.float32))
            y_out[section, c] = y.reshape(seqs, 2, cols)
        send_out(section)

    pltpu.make_async_copy(y_in, y_in, y_sem).wait()
    out_ref[...] = y_in[...]
    sent = x_ref.shape[0] - 1
    for i, ref in enumerate((f_ref, x_ref, y_in)):
        part = ref.at[pl.ds(0, sent)]
        pltpu.make_async_copy(part, part, send_sem.at[i]).wait()


def body(activations, short_filters, long_filters, skip_gain):
    tokens, width = activations.shape[1:]
    segs, seqs = lax.axis_size("segment"), lax.axis_size("seq")
    parts = segs * seqs
    mine = width // parts
    cols = COLS
    per = tokens // cols
    rows = 2 * per * seqs
    first = (lax.axis_index("seq") * segs + lax.axis_index("segment")) * mine
    taps = lax.dynamic_slice_in_dim(short_filters, first, mine, 2)
    taps = jnp.swapaxes(taps, 1, 2).reshape(2 * mine, -1).astype(jnp.float32)
    gains = lax.dynamic_slice_in_dim(skip_gain, first, mine, 1)

    def by_channel(block):
        return block.T.reshape(parts, mine, per, cols)

    scale = 1.0 / (rows * cols * math.sqrt(rows * cols // 2))
    tabs = tables(rows, cols)
    kept = tabs[4].shape[1]
    vm = pl.BlockSpec(memory_space=pltpu.VMEM)
    sm = pl.BlockSpec(memory_space=pltpu.SMEM)
    grid = pltpu.VMEM((2, mine, seqs, per, cols), jnp.bfloat16)
    chunks = pltpu.VMEM((parts, mine, per, cols), jnp.bfloat16)
    home = pl.pallas_call(
        functools.partial(kernel, scale, kept),
        out_shape=jax.ShapeDtypeStruct((parts, mine, per, cols), jnp.bfloat16),
        in_specs=[vm, vm, vm, sm, vm, vm, vm, vm, vm],
        out_specs=vm,
        scratch_shapes=[
            grid, grid, grid, chunks,
            pltpu.VMEM((2, mine, kept, 2 * cols), jnp.float32),
            pltpu.SemaphoreType.DMA((3,)), pltpu.SemaphoreType.DMA, pltpu.SemaphoreType.DMA,
            pltpu.SemaphoreType.DMA,
        ],
        compiler_params=pltpu.CompilerParams(
            vmem_limit_bytes=56 * 1024 * 1024, has_side_effects=True
        ),
    )(
        by_channel(activations[0]), by_channel(long_filters[0].astype(jnp.bfloat16)),
        taps, gains, *tabs,
    )
    return home.reshape(width, tokens).T[None]


def solution(mesh):
    return jax.shard_map(
        body,
        mesh=mesh,
        in_specs=(P("segment", "seq", None), P(), P("segment", "seq", None), P()),
        out_specs=P("segment", "seq", None),
        check_vma=False,
    )
```

```python
import functools
import math

import jax
import jax.numpy as jnp
import numpy as np
from jax import lax
from jax.experimental import pallas as pl
from jax.experimental.pallas import tpu as pltpu
from jax.sharding import PartitionSpec as P

MESH = pl.DeviceIdType.MESH
COLS = 128


def tables(rows, cols):
    half = rows // 2
    kept = (half + 1 + 15) // 16 * 16
    k1 = np.arange(kept)
    live = (k1 <= half).astype(np.float64)
    a = np.arange(half)
    ph = 2.0 * np.pi * ((k1[:, None] * a[None, :]) % rows) / rows
    row_fwd = np.concatenate([np.cos(ph) * live[:, None], -np.sin(ph) * live[:, None]], 0)
    weight = live * np.where((k1 == 0) | (k1 == half), 1.0, 2.0)
    row_back = np.concatenate([(np.cos(ph) * weight[:, None]).T, (-np.sin(ph) * weight[:, None]).T], 1)
    b = np.arange(cols)
    pc = 2.0 * np.pi * ((b[:, None] * b[None, :]) % cols) / cols
    c, s = np.cos(pc), np.sin(pc)
    col_fwd = np.block([[c, -s], [s, c]])
    col_back = np.block([[c, s], [-s, c]])
    tw = 2.0 * np.pi * ((k1[:, None] * b[None, :]) % (rows * cols)) / (rows * cols)
    bf = lambda x: jnp.asarray(x, jnp.bfloat16)
    return (
        bf(row_fwd), bf(row_back), bf(col_fwd), bf(col_back),
        jnp.asarray(np.stack([np.cos(tw), np.sin(tw)]), jnp.float32),
    )


def dot(a, b):
    return jnp.dot(a, b, preferred_element_type=jnp.float32)


def far_first(sizes):
    offsets = [(x, y, z) for x in range(sizes[0]) for y in range(sizes[1]) for z in range(sizes[2])]
    hops = lambda o: sum(min(d, n - d) for d, n in zip(o, sizes))
    return sorted(offsets, key=lambda o: (-hops(o), o))


def nt(a, b):
    return lax.dot_general(a, b, (((1,), (1,)), ((), ())), preferred_element_type=jnp.float32)


def tn(a, b):
    return lax.dot_general(a, b, (((0,), (0,)), ((), ())), preferred_element_type=jnp.float32)


def kernel(scale, kept, x_hbm, f_hbm, taps_hbm, gain_ref, rf_hbm, rb_hbm, cf_hbm, cb_hbm, tw_hbm,
           out_ref, x_raw, f_raw, taps_ref, rf_ref, rb_ref, cf_ref, cb_ref, tw_ref,
           both_send, both_in, y_out, y_in, spec,
           load_sem, send_sem, in_sem, y_sem):
    x_send, f_send = both_send.at[0], both_send.at[1]
    x_in, f_in = both_in.at[0], both_in.at[1]
    channels, seqs, cols = x_in.shape[1], x_in.shape[2], x_in.shape[4]
    width = x_send.shape[0]
    rows = 2 * seqs
    q, s = lax.axis_index("seq"), lax.axis_index("segment")
    mine = q * 2 + s
    xs = [lax.rem(q // 32 + d, 4) * 32 for d in range(4)]
    ys = [lax.rem(q // 8 + d, 4) * 8 for d in range(4)]
    zs = [lax.rem(q + d, 8) for d in range(8)]
    others = far_first((4, 4, 8))

    def seq_at(offset):
        return xs[offset[0]] + ys[offset[1]] + zs[offset[2]]

    def everyone(act):
        for offset in others:
            seq = seq_at(offset)
            act(seq, 1 - s)
            if any(offset):
                act(seq, s)

    loads = []
    for k, (a, b) in enumerate([
        (x_hbm, x_raw), (f_hbm, f_raw), (rf_hbm, rf_ref), (cf_hbm, cf_ref), (tw_hbm, tw_ref),
        (taps_hbm, taps_ref), (rb_hbm, rb_ref), (cb_hbm, cb_ref),
    ]):
        copy = pltpu.make_async_copy(a, b, load_sem.at[k])
        copy.start()
        loads.append(copy)

    barrier = pltpu.get_barrier_semaphore()
    everyone(lambda seq, core: pl.semaphore_signal(
        barrier, inc=1, device_id={"segment": core, "seq": seq}, device_id_type=MESH))

    weave = lax.broadcasted_iota(jnp.int32, (2 * cols, 2 * cols), 0)
    lane = lax.broadcasted_iota(jnp.int32, (2 * cols, 2 * cols), 1)
    weave = (lane == lax.rem(weave, 2) * cols + weave // 2).astype(jnp.float32).astype(jnp.bfloat16)

    def by_channel(raw, to_ref):
        for k in range(width // cols):
            block = raw[:, k * cols:(k + 1) * cols].astype(jnp.bfloat16)
            block = jnp.concatenate([block[:cols], block[cols:]], 1)
            woven = nt(weave, block).astype(jnp.bfloat16)
            to_ref[k * cols:(k + 1) * cols] = woven.reshape(cols, 2, cols)

    loads[1].wait()
    by_channel(f_raw, f_send)
    loads[0].wait()
    by_channel(x_raw, x_send)
    pl.semaphore_wait(barrier, 2 * seqs - 1)

    to_ref = both_in.at[:, s, :, q]
    everyone(lambda seq, core: pltpu.make_async_remote_copy(
        both_send.at[:, pl.ds((seq * 2 + core) * channels, channels)], to_ref,
        send_sem.at[0], in_sem, device_id={"segment": core, "seq": seq}, device_id_type=MESH,
    ).start())
    pltpu.make_async_copy(
        both_send.at[:, pl.ds(mine * channels, channels)], to_ref, in_sem
    ).start()

    def send_out(section):
        to_ref = y_in.at[pl.ds(mine * channels, channels)]

        def go(seq):
            pltpu.make_async_remote_copy(
                y_out.at[section, :, seq], to_ref, send_sem.at[1], y_sem,
                device_id={"segment": section, "seq": seq}, device_id_type=MESH,
            ).start()

        for offset in others:
            if any(offset):
                go(seq_at(offset))

        @pl.when(s == section)
        def _():
            pltpu.make_async_copy(y_out.at[section, :, q], to_ref, y_sem).start()

        @pl.when(s != section)
        def _():
            go(q)

    for copy in loads[2:]:
        copy.wait()
    first = mine * channels
    pick_c = lax.broadcasted_iota(jnp.int32, (16, width), 0)
    pick_l = lax.broadcasted_iota(jnp.int32, (16, width), 1)
    pick = (pick_l == first + pick_c).astype(jnp.float32)
    taps = [nt(pick.astype(jnp.bfloat16), taps_ref[section]) for section in range(2)]
    gains = [
        jnp.sum(jnp.where(pick > 0, gain_ref[section][None, :], 0.0), 1, keepdims=True)
        for section in range(2)
    ]

    b_in = lax.broadcasted_iota(jnp.int32, (cols, cols), 0)
    b_out = lax.broadcasted_iota(jnp.int32, (cols, cols), 1)
    top = lax.broadcasted_iota(jnp.int32, (rows, cols), 0) == 0

    def spectrum(grids):
        first = dot(rf_ref[...], jnp.concatenate(grids, 1))
        turned = []
        for c in range(len(grids)):
            re, im = first[:kept, c * cols:(c + 1) * cols], first[kept:, c * cols:(c + 1) * cols]
            cosine, sine = tw_ref[0], tw_ref[1]
            turned.append(jnp.concatenate(
                [re * cosine + im * sine, im * cosine - re * sine], 1
            ).astype(jnp.bfloat16))
        return [dot(t, cf_ref[...]) for t in turned]

    def inverse(products):
        turned = []
        for product in products:
            back = dot(product, cb_ref[...])
            re, im = back[:, :cols], back[:, cols:]
            cosine, sine = tw_ref[0], tw_ref[1]
            turned.append(jnp.concatenate(
                [re * cosine - im * sine, re * sine + im * cosine], 0
            ).astype(jnp.bfloat16))
        y = dot(rb_ref[...], jnp.concatenate(turned, 1)) * scale
        return [y[:, c * cols:(c + 1) * cols] for c in range(len(products))]

    def short(grid, taps):
        circ = pltpu.roll(jnp.broadcast_to(taps, (cols, cols)), 0, 1, stride=1, stride_axis=0)
        both = jnp.concatenate(
            [jnp.where(b_out >= b_in, circ, 0.0), jnp.where(b_out < b_in, circ, 0.0)], 0
        ).astype(jnp.bfloat16)
        earlier = jnp.where(top, 0.0, pltpu.roll(grid, 1, 0))
        return dot(jnp.concatenate([grid, earlier], 1).astype(jnp.bfloat16), both).astype(jnp.bfloat16)

    pltpu.make_async_copy(both_in, both_in, in_sem).wait()
    for section in range(2):
        got = spectrum([f_in[section, c].reshape(rows, cols) for c in range(channels)])
        for c in range(channels):
            spec[section, c] = got[c]

    previous = None
    for section in range(2):
        zs_now = []
        for c in range(channels):
            grid = x_in[section, c].reshape(rows, cols).astype(jnp.float32)
            if section:
                grid = (previous[c] * grid).astype(jnp.bfloat16).astype(jnp.float32)
            zs_now.append(short(grid, taps[section][c:c + 1]))
        products = []
        for c, signal in enumerate(spectrum(zs_now)):
            other = spec[section, c]
            ar, ai = signal[:, :cols], signal[:, cols:]
            hr, hi = other[:, :cols], other[:, cols:]
            products.append(
                jnp.concatenate([ar * hr - ai * hi, ar * hi + ai * hr], 1).astype(jnp.bfloat16)
            )
        previous = []
        for c, long in enumerate(inverse(products)):
            y = (
                long.astype(jnp.bfloat16).astype(jnp.float32)
                + gains[section][c:c + 1] * zs_now[c].astype(jnp.float32)
            ).astype(jnp.bfloat16)
            previous.append(y.astype(jnp.float32))
            y_out[section, c] = y.reshape(seqs, 2, cols)
        send_out(section)

    pltpu.make_async_copy(y_in, y_in, y_sem).wait()
    for k in range(width // cols):
        block = tn(y_in[k * cols:(k + 1) * cols].reshape(2 * cols, cols), weave).astype(jnp.bfloat16)
        out_ref[:cols, k * cols:(k + 1) * cols] = block[:, :cols]
        out_ref[cols:, k * cols:(k + 1) * cols] = block[:, cols:]
    part = both_send.at[:, pl.ds(0, width - channels)]
    pltpu.make_async_copy(part, part, send_sem.at[0]).wait()
    part = y_in.at[pl.ds(0, width - channels)]
    pltpu.make_async_copy(part, part, send_sem.at[1]).wait()


def body(activations, short_filters, long_filters, skip_gain):
    tokens, width = activations.shape[1:]
    segs, seqs = lax.axis_size("segment"), lax.axis_size("seq")
    mine = width // (segs * seqs)
    cols = COLS
    per = tokens // cols
    rows = 2 * per * seqs
    scale = 1.0 / (rows * cols * math.sqrt(rows * cols // 2))
    tabs = tables(rows, cols)
    kept = tabs[4].shape[1]
    vm = pl.BlockSpec(memory_space=pltpu.VMEM)
    far = pl.BlockSpec(memory_space=pl.ANY)
    grid = (2, mine, seqs, per, cols)
    chunks = (width, per, cols)
    vmem = lambda *shape: pltpu.VMEM(shape, jnp.bfloat16)
    like = lambda a: pltpu.VMEM(a.shape, a.dtype)
    x, f = activations[0], long_filters[0]
    dma = pltpu.SemaphoreType.DMA
    out = pl.pallas_call(
        functools.partial(kernel, scale, kept),
        out_shape=jax.ShapeDtypeStruct((tokens, width), jnp.bfloat16),
        in_specs=[far, far, far, vm, far, far, far, far, far],
        out_specs=vm,
        scratch_shapes=[
            like(x), like(f), like(short_filters), *[like(t) for t in tabs],
            vmem(2, *chunks), vmem(2, *grid), vmem(*grid), vmem(*chunks),
            pltpu.VMEM((2, mine, kept, 2 * cols), jnp.float32),
            dma((8,)), dma((2,)), dma, dma,
        ],
        compiler_params=pltpu.CompilerParams(
            vmem_limit_bytes=60 * 1024 * 1024, has_side_effects=True, collective_id=0
        ),
    )(x, f, short_filters, skip_gain, *tabs)
    return out[None]


def solution(mesh):
    return jax.shard_map(
        body,
        mesh=mesh,
        in_specs=(P("segment", "seq", None), P(), P("segment", "seq", None), P()),
        out_specs=P("segment", "seq", None),
        check_vma=False,
    )
```

```python
import functools
import math

import jax
import jax.numpy as jnp
import numpy as np
from jax import lax
from jax.experimental import pallas as pl
from jax.experimental.pallas import tpu as pltpu
from jax.sharding import PartitionSpec as P

MESH = pl.DeviceIdType.MESH
COLS = 128


def tables(rows, cols):
    half = rows // 2
    kept = (half + 1 + 15) // 16 * 16
    k1 = np.arange(kept)
    live = (k1 <= half).astype(np.float64)
    a = np.arange(half)
    ph = 2.0 * np.pi * ((k1[:, None] * a[None, :]) % rows) / rows
    row_fwd = np.concatenate([np.cos(ph) * live[:, None], -np.sin(ph) * live[:, None]], 0)
    weight = live * np.where((k1 == 0) | (k1 == half), 1.0, 2.0)
    row_back = np.concatenate([(np.cos(ph) * weight[:, None]).T, (-np.sin(ph) * weight[:, None]).T], 1)
    b = np.arange(cols)
    pc = 2.0 * np.pi * ((b[:, None] * b[None, :]) % cols) / cols
    c, s = np.cos(pc), np.sin(pc)
    col_fwd = np.block([[c, -s], [s, c]])
    col_back = np.block([[c, s], [-s, c]])
    tw = 2.0 * np.pi * ((k1[:, None] * b[None, :]) % (rows * cols)) / (rows * cols)
    bf = lambda x: jnp.asarray(x, jnp.bfloat16)
    return (
        bf(row_fwd), bf(row_back), bf(col_fwd), bf(col_back),
        jnp.asarray(np.stack([np.cos(tw), np.sin(tw)]), jnp.float32),
    )


def dot(a, b):
    return jnp.dot(a, b, preferred_element_type=jnp.float32)


def far_first(sizes):
    offsets = [(x, y, z) for x in range(sizes[0]) for y in range(sizes[1]) for z in range(sizes[2])]
    hops = lambda o: sum(min(d, n - d) for d, n in zip(o, sizes))
    return sorted(offsets, key=lambda o: (-hops(o), o))


def nt(a, b):
    return lax.dot_general(a, b, (((1,), (1,)), ((), ())), preferred_element_type=jnp.float32)


def tn(a, b):
    return lax.dot_general(a, b, (((0,), (0,)), ((), ())), preferred_element_type=jnp.float32)


def kernel(scale, kept, x_hbm, f_hbm, taps_hbm, gain_hbm, rf_hbm, rb_hbm, cf_hbm, cb_hbm, tw_hbm,
           out_ref, x_raw, f_raw, taps_ref, gain_ref, rf_ref, rb_ref, cf_ref, cb_ref, tw_ref,
           both_send, both_in, y_out, y_in, spec, toeplitz,
           load_sem, send_sem, in_sems, y_sem):
    x_send, f_send = both_send.at[0], both_send.at[1]
    x_in, f_in = both_in.at[0], both_in.at[1]
    channels, seqs, cols = x_in.shape[1], x_in.shape[2], x_in.shape[4]
    width = x_send.shape[0]
    rows = 2 * seqs
    q, s = lax.axis_index("seq"), lax.axis_index("segment")
    mine = q * 2 + s
    xs = [lax.rem(q // 32 + d, 4) * 32 for d in range(4)]
    ys = [lax.rem(q // 8 + d, 4) * 8 for d in range(4)]
    zs = [lax.rem(q + d, 8) for d in range(8)]
    others = far_first((4, 4, 8))

    def seq_at(offset):
        return xs[offset[0]] + ys[offset[1]] + zs[offset[2]]

    def everyone(act):
        for offset in others:
            seq = seq_at(offset)
            act(seq, 1 - s)
            if any(offset):
                act(seq, s)

    loads = []
    for k, (a, b) in enumerate([
        (x_hbm, x_raw), (f_hbm, f_raw), (rf_hbm, rf_ref), (cf_hbm, cf_ref), (tw_hbm, tw_ref),
        (taps_hbm, taps_ref), (rb_hbm, rb_ref), (cb_hbm, cb_ref),
        (gain_hbm, gain_ref),
    ]):
        copy = pltpu.make_async_copy(a, b, load_sem.at[k])
        copy.start()
        loads.append(copy)

    barrier = pltpu.get_barrier_semaphore()
    everyone(lambda seq, core: pl.semaphore_signal(
        barrier, inc=1, device_id={"segment": core, "seq": seq}, device_id_type=MESH))

    weave = lax.broadcasted_iota(jnp.int32, (2 * cols, 2 * cols), 0)
    lane = lax.broadcasted_iota(jnp.int32, (2 * cols, 2 * cols), 1)
    weave = (lane == lax.rem(weave, 2) * cols + weave // 2).astype(jnp.float32).astype(jnp.bfloat16)

    def by_channel(raw, to_ref):
        for k in range(width // cols):
            block = raw[:, k * cols:(k + 1) * cols].astype(jnp.bfloat16)
            block = jnp.concatenate([block[:cols], block[cols:]], 1)
            woven = nt(weave, block).astype(jnp.bfloat16)
            to_ref[k * cols:(k + 1) * cols] = woven.reshape(cols, 2, cols)

    loads[1].wait()
    by_channel(f_raw, f_send)
    loads[0].wait()
    by_channel(x_raw, x_send)
    pl.semaphore_wait(barrier, 2 * seqs - 1)

    in_sem = in_sems.at[s]
    to_ref = both_in.at[:, s, :, q]
    everyone(lambda seq, core: pltpu.make_async_remote_copy(
        both_send.at[:, pl.ds((seq * 2 + core) * channels, channels)], to_ref,
        send_sem.at[0], in_sem, device_id={"segment": core, "seq": seq}, device_id_type=MESH,
    ).start())
    pltpu.make_async_copy(
        both_send.at[:, pl.ds(mine * channels, channels)], to_ref, in_sem
    ).start()

    def send_out(section):
        to_ref = y_in.at[pl.ds(mine * channels, channels)]

        def go(seq):
            pltpu.make_async_remote_copy(
                y_out.at[section, :, seq], to_ref, send_sem.at[1], y_sem,
                device_id={"segment": section, "seq": seq}, device_id_type=MESH,
            ).start()

        for offset in others:
            if any(offset):
                go(seq_at(offset))

        @pl.when(s == section)
        def _():
            pltpu.make_async_copy(y_out.at[section, :, q], to_ref, y_sem).start()

        @pl.when(s != section)
        def _():
            go(q)

    for copy in loads[2:]:
        copy.wait()
    first = mine * channels
    pick_c = lax.broadcasted_iota(jnp.int32, (16, width), 0)
    pick_l = lax.broadcasted_iota(jnp.int32, (16, width), 1)
    pick = (pick_l == first + pick_c).astype(jnp.float32)
    taps = [nt(pick.astype(jnp.bfloat16), taps_ref[section]) for section in range(2)]
    gains = [
        jnp.sum(jnp.where(pick > 0, gain_ref[section][None, :], 0.0), 1, keepdims=True)
        for section in range(2)
    ]

    b_in = lax.broadcasted_iota(jnp.int32, (cols, cols), 0)
    b_out = lax.broadcasted_iota(jnp.int32, (cols, cols), 1)
    top = lax.broadcasted_iota(jnp.int32, (rows, cols), 0) == 0

    def spectrum(grids):
        first = dot(rf_ref[...], jnp.concatenate(grids, 1))
        turned = []
        for c in range(len(grids)):
            re, im = first[:kept, c * cols:(c + 1) * cols], first[kept:, c * cols:(c + 1) * cols]
            cosine, sine = tw_ref[0], tw_ref[1]
            turned.append(jnp.concatenate(
                [re * cosine + im * sine, im * cosine - re * sine], 1
            ).astype(jnp.bfloat16))
        return [dot(t, cf_ref[...]) for t in turned]

    def inverse(products):
        turned = []
        for product in products:
            back = dot(product, cb_ref[...])
            re, im = back[:, :cols], back[:, cols:]
            cosine, sine = tw_ref[0], tw_ref[1]
            turned.append(jnp.concatenate(
                [re * cosine - im * sine, re * sine + im * cosine], 0
            ).astype(jnp.bfloat16))
        y = dot(rb_ref[...], jnp.concatenate(turned, 1)) * scale
        return [y[:, c * cols:(c + 1) * cols] for c in range(len(products))]

    def short(grid, section, c):
        earlier = jnp.where(top, 0.0, pltpu.roll(grid, 1, 0))
        both = jnp.concatenate([grid, earlier], 1).astype(jnp.bfloat16)
        return dot(both, toeplitz[section, c]).astype(jnp.bfloat16)

    for section in range(2):
        for c in range(channels):
            circ = pltpu.roll(
                jnp.broadcast_to(taps[section][c:c + 1], (cols, cols)), 0, 1, stride=1, stride_axis=0
            )
            toeplitz[section, c] = jnp.concatenate(
                [jnp.where(b_out >= b_in, circ, 0.0), jnp.where(b_out < b_in, circ, 0.0)], 0
            ).astype(jnp.bfloat16)

    previous = None
    for section in range(2):
        part = both_in.at[:, section]
        pltpu.make_async_copy(part, part, in_sems.at[section]).wait()
        got = spectrum([f_in[section, c].reshape(rows, cols) for c in range(channels)])
        for c in range(channels):
            spec[section, c] = got[c]
        zs_now = []
        for c in range(channels):
            grid = x_in[section, c].reshape(rows, cols).astype(jnp.float32)
            if section:
                grid = (previous[c] * grid).astype(jnp.bfloat16).astype(jnp.float32)
            zs_now.append(short(grid, section, c))
        products = []
        for c, signal in enumerate(spectrum(zs_now)):
            other = spec[section, c]
            ar, ai = signal[:, :cols], signal[:, cols:]
            hr, hi = other[:, :cols], other[:, cols:]
            products.append(
                jnp.concatenate([ar * hr - ai * hi, ar * hi + ai * hr], 1).astype(jnp.bfloat16)
            )
        previous = []
        for c, long in enumerate(inverse(products)):
            y = (
                long.astype(jnp.bfloat16).astype(jnp.float32)
                + gains[section][c:c + 1] * zs_now[c].astype(jnp.float32)
            ).astype(jnp.bfloat16)
            previous.append(y.astype(jnp.float32))
            y_out[section, c] = y.reshape(seqs, 2, cols)
        send_out(section)

    pltpu.make_async_copy(y_in, y_in, y_sem).wait()
    for k in range(width // cols):
        block = tn(y_in[k * cols:(k + 1) * cols].reshape(2 * cols, cols), weave).astype(jnp.bfloat16)
        out_ref[:cols, k * cols:(k + 1) * cols] = block[:, :cols]
        out_ref[cols:, k * cols:(k + 1) * cols] = block[:, cols:]
    part = both_send.at[:, pl.ds(0, width - channels)]
    pltpu.make_async_copy(part, part, send_sem.at[0]).wait()
    part = y_in.at[pl.ds(0, width - channels)]
    pltpu.make_async_copy(part, part, send_sem.at[1]).wait()


def body(activations, short_filters, long_filters, skip_gain):
    tokens, width = activations.shape[1:]
    segs, seqs = lax.axis_size("segment"), lax.axis_size("seq")
    mine = width // (segs * seqs)
    cols = COLS
    per = tokens // cols
    rows = 2 * per * seqs
    scale = 1.0 / (rows * cols * math.sqrt(rows * cols // 2))
    tabs = tables(rows, cols)
    kept = tabs[4].shape[1]
    vm = pl.BlockSpec(memory_space=pltpu.VMEM)
    far = pl.BlockSpec(memory_space=pl.ANY)
    grid = (2, mine, seqs, per, cols)
    chunks = (width, per, cols)
    vmem = lambda *shape: pltpu.VMEM(shape, jnp.bfloat16)
    like = lambda a: pltpu.VMEM(a.shape, a.dtype)
    x, f = activations[0], long_filters[0]
    dma = pltpu.SemaphoreType.DMA
    out = pl.pallas_call(
        functools.partial(kernel, scale, kept),
        out_shape=pltpu.VMEM((tokens, width), jnp.bfloat16),
        in_specs=[far] * 9,
        out_specs=vm,
        scratch_shapes=[
            like(x), like(f), like(short_filters), like(skip_gain), *[like(t) for t in tabs],
            vmem(2, *chunks), vmem(2, *grid), vmem(*grid), vmem(*chunks),
            pltpu.VMEM((2, mine, kept, 2 * cols), jnp.float32), vmem(2, mine, 2 * cols, cols),
            dma((9,)), dma((2,)), dma((2,)), dma,
        ],
        compiler_params=pltpu.CompilerParams(
            vmem_limit_bytes=54900 * 1024, has_side_effects=True, collective_id=0
        ),
    )(x, f, short_filters, skip_gain, *tabs)
    return out[None]


def solution(mesh):
    return jax.shard_map(
        body,
        mesh=mesh,
        in_specs=(P("segment", "seq", None), P(), P("segment", "seq", None), P()),
        out_specs=P("segment", "seq", None),
        check_vma=False,
    )
```

```python
import functools
import math

import jax
import jax.numpy as jnp
import numpy as np
from jax import lax
from jax.experimental import pallas as pl
from jax.experimental.pallas import tpu as pltpu
from jax.sharding import PartitionSpec as P

MESH = pl.DeviceIdType.MESH
COLS = 128
AHEAD = 12


def tables(rows, cols):
    half = rows // 2
    kept = (half + 1 + 15) // 16 * 16
    k1 = np.arange(kept)
    live = (k1 <= half).astype(np.float64)
    a = np.arange(half)
    ph = 2.0 * np.pi * ((k1[:, None] * a[None, :]) % rows) / rows
    row_fwd = np.concatenate([np.cos(ph) * live[:, None], -np.sin(ph) * live[:, None]], 0)
    weight = live * np.where((k1 == 0) | (k1 == half), 1.0, 2.0)
    row_back = np.concatenate([(np.cos(ph) * weight[:, None]).T, (-np.sin(ph) * weight[:, None]).T], 1)
    b = np.arange(cols)
    pc = 2.0 * np.pi * ((b[:, None] * b[None, :]) % cols) / cols
    c, s = np.cos(pc), np.sin(pc)
    col_fwd = np.block([[c, -s], [s, c]])
    col_back = np.block([[c, s], [-s, c]])
    tw = 2.0 * np.pi * ((k1[:, None] * b[None, :]) % (rows * cols)) / (rows * cols)
    bf = lambda x: jnp.asarray(x, jnp.bfloat16)
    return (
        bf(row_fwd), bf(row_back), bf(col_fwd), bf(col_back),
        jnp.asarray(np.stack([np.cos(tw), np.sin(tw)]), jnp.float32),
    )


def dot(a, b):
    return jnp.dot(a, b, preferred_element_type=jnp.float32)


def far_first(sizes):
    offsets = [(x, y, z) for x in range(sizes[0]) for y in range(sizes[1]) for z in range(sizes[2])]
    hops = lambda o: sum(min(d, n - d) for d, n in zip(o, sizes))
    return sorted(offsets, key=lambda o: (-hops(o), o))


def nt(a, b):
    return lax.dot_general(a, b, (((1,), (1,)), ((), ())), preferred_element_type=jnp.float32)


def tn(a, b):
    return lax.dot_general(a, b, (((0,), (0,)), ((), ())), preferred_element_type=jnp.float32)


def kernel(scale, kept, x_hbm, f_hbm, taps_hbm, gain_hbm, rf_hbm, rb_hbm, cf_hbm, cb_hbm, tw_hbm,
           out_ref, x_raw, f_raw, taps_ref, gain_ref, rf_ref, rb_ref, cf_ref, cb_ref, tw_ref,
           both_send, both_in, y_out, y_in, spec, toeplitz,
           load_sem, send_sem, in_sems, y_sem):
    x_send, f_send = both_send.at[0], both_send.at[1]
    x_in, f_in = both_in.at[0], both_in.at[1]
    channels, seqs, cols = x_in.shape[1], x_in.shape[2], x_in.shape[4]
    width = x_send.shape[0]
    rows = 2 * seqs
    q, s = lax.axis_index("seq"), lax.axis_index("segment")
    mine = q * 2 + s
    xs = [lax.rem(q // 32 + d, 4) * 32 for d in range(4)]
    ys = [lax.rem(q // 8 + d, 4) * 8 for d in range(4)]
    zs = [lax.rem(q + d, 8) for d in range(8)]
    others = far_first((4, 4, 8))
    ahead = AHEAD

    def seq_at(offset):
        return xs[offset[0]] + ys[offset[1]] + zs[offset[2]]

    def everyone(act):
        for offset in others:
            seq = seq_at(offset)
            act(seq, 1 - s)
            if any(offset):
                act(seq, s)

    loads = []
    for k, (a, b) in enumerate([
        (x_hbm, x_raw), (f_hbm, f_raw), (rf_hbm, rf_ref), (cf_hbm, cf_ref), (tw_hbm, tw_ref),
        (taps_hbm, taps_ref), (rb_hbm, rb_ref), (cb_hbm, cb_ref),
        (gain_hbm, gain_ref),
    ]):
        copy = pltpu.make_async_copy(a, b, load_sem.at[k])
        copy.start()
        loads.append(copy)

    barrier = pltpu.get_barrier_semaphore()
    everyone(lambda seq, core: pl.semaphore_signal(
        barrier, inc=1, device_id={"segment": core, "seq": seq}, device_id_type=MESH))

    weave = lax.broadcasted_iota(jnp.int32, (2 * cols, 2 * cols), 0)
    lane = lax.broadcasted_iota(jnp.int32, (2 * cols, 2 * cols), 1)
    weave = (lane == lax.rem(weave, 2) * cols + weave // 2).astype(jnp.float32).astype(jnp.bfloat16)

    def by_channel(raw, to_ref):
        for k in range(width // cols):
            block = raw[:, k * cols:(k + 1) * cols].astype(jnp.bfloat16)
            block = jnp.concatenate([block[:cols], block[cols:]], 1)
            woven = nt(weave, block).astype(jnp.bfloat16)
            to_ref[k * cols:(k + 1) * cols] = woven.reshape(cols, 2, cols)

    loads[1].wait()
    by_channel(f_raw, f_send)
    loads[0].wait()
    by_channel(x_raw, x_send)
    pl.semaphore_wait(barrier, 2 * seqs - 1)

    to_ref = both_in.at[:, s, :, q]

    def send_in(offsets, sem):
        def go(seq, core):
            pltpu.make_async_remote_copy(
                both_send.at[:, pl.ds((seq * 2 + core) * channels, channels)], to_ref,
                send_sem.at[0], sem, device_id={"segment": core, "seq": seq}, device_id_type=MESH,
            ).start()

        for offset in offsets:
            seq = seq_at(offset)
            go(seq, 1 - s)
            if any(offset):
                go(seq, s)
            else:
                pltpu.make_async_copy(
                    both_send.at[:, pl.ds(mine * channels, channels)], to_ref, sem
                ).start()

    def wait_in(section, count, sem):
        part = both_in.at[:, section, :, pl.ds(0, count)]
        pltpu.make_async_copy(part, part, sem).wait()

    @pl.when(s == 0)
    def _():
        send_in(others[:ahead], in_sems.at[0])
        send_in(others[ahead:], in_sems.at[1])

    def send_out(section):
        to_ref = y_in.at[pl.ds(mine * channels, channels)]

        def go(seq):
            pltpu.make_async_remote_copy(
                y_out.at[section, :, seq], to_ref, send_sem.at[1], y_sem,
                device_id={"segment": section, "seq": seq}, device_id_type=MESH,
            ).start()

        for offset in others:
            if any(offset):
                go(seq_at(offset))

        @pl.when(s == section)
        def _():
            pltpu.make_async_copy(y_out.at[section, :, q], to_ref, y_sem).start()

        @pl.when(s != section)
        def _():
            go(q)

    for copy in loads[2:]:
        copy.wait()
    first = mine * channels
    pick_c = lax.broadcasted_iota(jnp.int32, (16, width), 0)
    pick_l = lax.broadcasted_iota(jnp.int32, (16, width), 1)
    pick = (pick_l == first + pick_c).astype(jnp.float32)
    taps = [nt(pick.astype(jnp.bfloat16), taps_ref[section]) for section in range(2)]
    gains = [
        jnp.sum(jnp.where(pick > 0, gain_ref[section][None, :], 0.0), 1, keepdims=True)
        for section in range(2)
    ]

    b_in = lax.broadcasted_iota(jnp.int32, (cols, cols), 0)
    b_out = lax.broadcasted_iota(jnp.int32, (cols, cols), 1)
    top = lax.broadcasted_iota(jnp.int32, (rows, cols), 0) == 0

    def spectrum(grids):
        first = dot(rf_ref[...], jnp.concatenate(grids, 1))
        turned = []
        for c in range(len(grids)):
            re, im = first[:kept, c * cols:(c + 1) * cols], first[kept:, c * cols:(c + 1) * cols]
            cosine, sine = tw_ref[0], tw_ref[1]
            turned.append(jnp.concatenate(
                [re * cosine + im * sine, im * cosine - re * sine], 1
            ).astype(jnp.bfloat16))
        return [dot(t, cf_ref[...]) for t in turned]

    def inverse(products):
        turned = []
        for product in products:
            back = dot(product, cb_ref[...])
            re, im = back[:, :cols], back[:, cols:]
            cosine, sine = tw_ref[0], tw_ref[1]
            turned.append(jnp.concatenate(
                [re * cosine - im * sine, re * sine + im * cosine], 0
            ).astype(jnp.bfloat16))
        y = dot(rb_ref[...], jnp.concatenate(turned, 1)) * scale
        return [y[:, c * cols:(c + 1) * cols] for c in range(len(products))]

    def short(grid, section, c):
        earlier = jnp.where(top, 0.0, pltpu.roll(grid, 1, 0))
        both = jnp.concatenate([grid, earlier], 1).astype(jnp.bfloat16)
        return dot(both, toeplitz[section, c]).astype(jnp.bfloat16)

    for section in range(2):
        for c in range(channels):
            circ = pltpu.roll(
                jnp.broadcast_to(taps[section][c:c + 1], (cols, cols)), 0, 1, stride=1, stride_axis=0
            )
            toeplitz[section, c] = jnp.concatenate(
                [jnp.where(b_out >= b_in, circ, 0.0), jnp.where(b_out < b_in, circ, 0.0)], 0
            ).astype(jnp.bfloat16)

    wait_in(0, ahead, in_sems.at[0])

    @pl.when(s == 1)
    def _():
        send_in(others, in_sems.at[2])

    previous = None
    for section in range(2):
        wait_in(section, seqs if section else seqs - ahead, in_sems.at[1 + section])
        got = spectrum([f_in[section, c].reshape(rows, cols) for c in range(channels)])
        for c in range(channels):
            spec[section, c] = got[c]
        zs_now = []
        for c in range(channels):
            grid = x_in[section, c].reshape(rows, cols).astype(jnp.float32)
            if section:
                grid = (previous[c] * grid).astype(jnp.bfloat16).astype(jnp.float32)
            zs_now.append(short(grid, section, c))
        products = []
        for c, signal in enumerate(spectrum(zs_now)):
            other = spec[section, c]
            ar, ai = signal[:, :cols], signal[:, cols:]
            hr, hi = other[:, :cols], other[:, cols:]
            products.append(
                jnp.concatenate([ar * hr - ai * hi, ar * hi + ai * hr], 1).astype(jnp.bfloat16)
            )
        previous = []
        for c, long in enumerate(inverse(products)):
            y = (
                long.astype(jnp.bfloat16).astype(jnp.float32)
                + gains[section][c:c + 1] * zs_now[c].astype(jnp.float32)
            ).astype(jnp.bfloat16)
            previous.append(y.astype(jnp.float32))
            y_out[section, c] = y.reshape(seqs, 2, cols)
        send_out(section)

    pltpu.make_async_copy(y_in, y_in, y_sem).wait()
    for k in range(width // cols):
        block = tn(y_in[k * cols:(k + 1) * cols].reshape(2 * cols, cols), weave).astype(jnp.bfloat16)
        out_ref[:cols, k * cols:(k + 1) * cols] = block[:, :cols]
        out_ref[cols:, k * cols:(k + 1) * cols] = block[:, cols:]
    part = both_send.at[:, pl.ds(0, width - channels)]
    pltpu.make_async_copy(part, part, send_sem.at[0]).wait()
    part = y_in.at[pl.ds(0, width - channels)]
    pltpu.make_async_copy(part, part, send_sem.at[1]).wait()


def body(activations, short_filters, long_filters, skip_gain):
    tokens, width = activations.shape[1:]
    segs, seqs = lax.axis_size("segment"), lax.axis_size("seq")
    mine = width // (segs * seqs)
    cols = COLS
    per = tokens // cols
    rows = 2 * per * seqs
    scale = 1.0 / (rows * cols * math.sqrt(rows * cols // 2))
    tabs = tables(rows, cols)
    kept = tabs[4].shape[1]
    vm = pl.BlockSpec(memory_space=pltpu.VMEM)
    far = pl.BlockSpec(memory_space=pl.ANY)
    grid = (2, mine, seqs, per, cols)
    chunks = (width, per, cols)
    vmem = lambda *shape: pltpu.VMEM(shape, jnp.bfloat16)
    like = lambda a: pltpu.VMEM(a.shape, a.dtype)
    x, f = activations[0], long_filters[0]
    dma = pltpu.SemaphoreType.DMA
    out = pl.pallas_call(
        functools.partial(kernel, scale, kept),
        out_shape=pltpu.VMEM((tokens, width), jnp.bfloat16),
        in_specs=[far] * 9,
        out_specs=vm,
        scratch_shapes=[
            like(x), like(f), like(short_filters), like(skip_gain), *[like(t) for t in tabs],
            vmem(2, *chunks), vmem(2, *grid), vmem(*grid), vmem(*chunks),
            pltpu.VMEM((2, mine, kept, 2 * cols), jnp.float32), vmem(2, mine, 2 * cols, cols),
            dma((9,)), dma((2,)), dma((3,)), dma,
        ],
        compiler_params=pltpu.CompilerParams(
            vmem_limit_bytes=54900 * 1024, has_side_effects=True, collective_id=0
        ),
    )(x, f, short_filters, skip_gain, *tabs)
    return out[None]


def solution(mesh):
    return jax.shard_map(
        body,
        mesh=mesh,
        in_specs=(P("segment", "seq", None), P(), P("segment", "seq", None), P()),
        out_specs=P("segment", "seq", None),
        check_vma=False,
    )
```

```python
import functools
import math

import jax
import jax.numpy as jnp
import numpy as np
from jax import lax
from jax.experimental import pallas as pl
from jax.experimental.pallas import tpu as pltpu
from jax.sharding import PartitionSpec as P

MESH = pl.DeviceIdType.MESH
COLS = 128
AHEAD = 12


def tables(rows, cols):
    half = rows // 2
    kept = (half + 1 + 15) // 16 * 16
    k1 = np.arange(kept)
    live = (k1 <= half).astype(np.float64)
    a = np.arange(half)
    ph = 2.0 * np.pi * ((k1[:, None] * a[None, :]) % rows) / rows
    row_fwd = np.concatenate([np.cos(ph) * live[:, None], -np.sin(ph) * live[:, None]], 0)
    weight = live * np.where((k1 == 0) | (k1 == half), 1.0, 2.0)
    row_back = np.concatenate([(np.cos(ph) * weight[:, None]).T, (-np.sin(ph) * weight[:, None]).T], 1)
    b = np.arange(cols)
    pc = 2.0 * np.pi * ((b[:, None] * b[None, :]) % cols) / cols
    c, s = np.cos(pc), np.sin(pc)
    col_fwd = np.block([[c, -s], [s, c]])
    col_back = np.block([[c, s], [-s, c]])
    tw = 2.0 * np.pi * ((k1[:, None] * b[None, :]) % (rows * cols)) / (rows * cols)
    bf = lambda x: jnp.asarray(x, jnp.bfloat16)
    return (
        bf(row_fwd), bf(row_back), bf(col_fwd), bf(col_back),
        jnp.asarray(np.stack([np.cos(tw), np.sin(tw)]), jnp.float32),
    )


def dot(a, b):
    return jnp.dot(a, b, preferred_element_type=jnp.float32)


def far_first(sizes):
    offsets = [(x, y, z) for x in range(sizes[0]) for y in range(sizes[1]) for z in range(sizes[2])]
    hops = lambda o: sum(min(d, n - d) for d, n in zip(o, sizes))
    return sorted(offsets, key=lambda o: (-hops(o), o[::-1]))


def nt(a, b):
    return lax.dot_general(a, b, (((1,), (1,)), ((), ())), preferred_element_type=jnp.float32)


def tn(a, b):
    return lax.dot_general(a, b, (((0,), (0,)), ((), ())), preferred_element_type=jnp.float32)


def kernel(scale, kept, x_hbm, f_hbm, taps_hbm, gain_hbm, rf_hbm, rb_hbm, cf_hbm, cb_hbm, tw_hbm,
           out_ref, x_raw, f_raw, taps_ref, gain_ref, rf_ref, rb_ref, cf_ref, cb_ref, tw_ref,
           both_send, both_in, y_out, y_in, spec, toeplitz,
           load_sem, send_sem, in_sems, y_sem):
    x_send, f_send = both_send.at[0], both_send.at[1]
    x_in, f_in = both_in.at[0], both_in.at[1]
    channels, seqs, cols = x_in.shape[1], x_in.shape[2], x_in.shape[4]
    width = x_send.shape[0]
    rows = 2 * seqs
    q, s = lax.axis_index("seq"), lax.axis_index("segment")
    mine = q * 2 + s
    xs = [lax.rem(q // 32 + d, 4) * 32 for d in range(4)]
    ys = [lax.rem(q // 8 + d, 4) * 8 for d in range(4)]
    zs = [lax.rem(q + d, 8) for d in range(8)]
    others = far_first((4, 4, 8))
    ahead = AHEAD

    def seq_at(offset):
        return xs[offset[0]] + ys[offset[1]] + zs[offset[2]]

    def everyone(act):
        for offset in others:
            seq = seq_at(offset)
            act(seq, 1 - s)
            if any(offset):
                act(seq, s)

    loads = []
    for k, (a, b) in enumerate([
        (x_hbm, x_raw), (f_hbm, f_raw), (rf_hbm, rf_ref), (cf_hbm, cf_ref), (tw_hbm, tw_ref),
        (taps_hbm, taps_ref), (rb_hbm, rb_ref), (cb_hbm, cb_ref),
        (gain_hbm, gain_ref),
    ]):
        copy = pltpu.make_async_copy(a, b, load_sem.at[k])
        copy.start()
        loads.append(copy)

    barrier = pltpu.get_barrier_semaphore()
    everyone(lambda seq, core: pl.semaphore_signal(
        barrier, inc=1, device_id={"segment": core, "seq": seq}, device_id_type=MESH))

    weave = lax.broadcasted_iota(jnp.int32, (2 * cols, 2 * cols), 0)
    lane = lax.broadcasted_iota(jnp.int32, (2 * cols, 2 * cols), 1)
    weave = (lane == lax.rem(weave, 2) * cols + weave // 2).astype(jnp.float32).astype(jnp.bfloat16)

    def by_channel(raw, to_ref):
        for k in range(width // cols):
            block = raw[:, k * cols:(k + 1) * cols].astype(jnp.bfloat16)
            block = jnp.concatenate([block[:cols], block[cols:]], 1)
            woven = nt(weave, block).astype(jnp.bfloat16)
            to_ref[k * cols:(k + 1) * cols] = woven.reshape(cols, 2, cols)

    loads[1].wait()
    by_channel(f_raw, f_send)
    loads[0].wait()
    by_channel(x_raw, x_send)
    pl.semaphore_wait(barrier, 2 * seqs - 1)

    to_ref = both_in.at[:, s, :, q]

    def send_in(offsets, sem):
        def go(seq, core):
            pltpu.make_async_remote_copy(
                both_send.at[:, pl.ds((seq * 2 + core) * channels, channels)], to_ref,
                send_sem.at[0], sem, device_id={"segment": core, "seq": seq}, device_id_type=MESH,
            ).start()

        for offset in offsets:
            seq = seq_at(offset)
            go(seq, 1 - s)
            if any(offset):
                go(seq, s)
            else:
                pltpu.make_async_copy(
                    both_send.at[:, pl.ds(mine * channels, channels)], to_ref, sem
                ).start()

    def wait_in(section, count, sem):
        part = both_in.at[:, section, :, pl.ds(0, count)]
        pltpu.make_async_copy(part, part, sem).wait()

    @pl.when(s == 0)
    def _():
        send_in(others[:ahead], in_sems.at[0])
        send_in(others[ahead:], in_sems.at[1])

    def send_out(section):
        to_ref = y_in.at[pl.ds(mine * channels, channels)]

        def go(seq):
            pltpu.make_async_remote_copy(
                y_out.at[section, :, seq], to_ref, send_sem.at[1], y_sem,
                device_id={"segment": section, "seq": seq}, device_id_type=MESH,
            ).start()

        for offset in others:
            if any(offset):
                go(seq_at(offset))

        @pl.when(s == section)
        def _():
            pltpu.make_async_copy(y_out.at[section, :, q], to_ref, y_sem).start()

        @pl.when(s != section)
        def _():
            go(q)

    for copy in loads[2:]:
        copy.wait()
    first = mine * channels
    pick_c = lax.broadcasted_iota(jnp.int32, (16, width), 0)
    pick_l = lax.broadcasted_iota(jnp.int32, (16, width), 1)
    pick = (pick_l == first + pick_c).astype(jnp.float32)
    taps = [nt(pick.astype(jnp.bfloat16), taps_ref[section]) for section in range(2)]
    gains = [
        jnp.sum(jnp.where(pick > 0, gain_ref[section][None, :], 0.0), 1, keepdims=True)
        for section in range(2)
    ]

    b_in = lax.broadcasted_iota(jnp.int32, (cols, cols), 0)
    b_out = lax.broadcasted_iota(jnp.int32, (cols, cols), 1)
    top = lax.broadcasted_iota(jnp.int32, (rows, cols), 0) == 0

    def spectrum(grids):
        first = dot(rf_ref[...], jnp.concatenate(grids, 1))
        turned = []
        for c in range(len(grids)):
            re, im = first[:kept, c * cols:(c + 1) * cols], first[kept:, c * cols:(c + 1) * cols]
            cosine, sine = tw_ref[0], tw_ref[1]
            turned.append(jnp.concatenate(
                [re * cosine + im * sine, im * cosine - re * sine], 1
            ).astype(jnp.bfloat16))
        return [dot(t, cf_ref[...]) for t in turned]

    def inverse(products):
        turned = []
        for product in products:
            back = dot(product, cb_ref[...])
            re, im = back[:, :cols], back[:, cols:]
            cosine, sine = tw_ref[0], tw_ref[1]
            turned.append(jnp.concatenate(
                [re * cosine - im * sine, re * sine + im * cosine], 0
            ).astype(jnp.bfloat16))
        y = dot(rb_ref[...], jnp.concatenate(turned, 1)) * scale
        return [y[:, c * cols:(c + 1) * cols] for c in range(len(products))]

    def short(grid, section, c):
        earlier = jnp.where(top, 0.0, pltpu.roll(grid, 1, 0))
        both = jnp.concatenate([grid, earlier], 1).astype(jnp.bfloat16)
        return dot(both, toeplitz[section, c]).astype(jnp.bfloat16)

    for section in range(2):
        for c in range(channels):
            circ = pltpu.roll(
                jnp.broadcast_to(taps[section][c:c + 1], (cols, cols)), 0, 1, stride=1, stride_axis=0
            )
            toeplitz[section, c] = jnp.concatenate(
                [jnp.where(b_out >= b_in, circ, 0.0), jnp.where(b_out < b_in, circ, 0.0)], 0
            ).astype(jnp.bfloat16)

    wait_in(0, ahead, in_sems.at[0])

    @pl.when(s == 1)
    def _():
        send_in(others, in_sems.at[2])

    previous = None
    for section in range(2):
        wait_in(section, seqs if section else seqs - ahead, in_sems.at[1 + section])
        got = spectrum([f_in[section, c].reshape(rows, cols) for c in range(channels)])
        for c in range(channels):
            spec[section, c] = got[c]
        zs_now = []
        for c in range(channels):
            grid = x_in[section, c].reshape(rows, cols).astype(jnp.float32)
            if section:
                grid = (previous[c] * grid).astype(jnp.bfloat16).astype(jnp.float32)
            zs_now.append(short(grid, section, c))
        products = []
        for c, signal in enumerate(spectrum(zs_now)):
            other = spec[section, c]
            ar, ai = signal[:, :cols], signal[:, cols:]
            hr, hi = other[:, :cols], other[:, cols:]
            products.append(
                jnp.concatenate([ar * hr - ai * hi, ar * hi + ai * hr], 1).astype(jnp.bfloat16)
            )
        previous = []
        for c, long in enumerate(inverse(products)):
            y = (
                long.astype(jnp.bfloat16).astype(jnp.float32)
                + gains[section][c:c + 1] * zs_now[c].astype(jnp.float32)
            ).astype(jnp.bfloat16)
            previous.append(y.astype(jnp.float32))
            y_out[section, c] = y.reshape(seqs, 2, cols)
        send_out(section)

    pltpu.make_async_copy(y_in, y_in, y_sem).wait()
    for k in range(width // cols):
        block = tn(y_in[k * cols:(k + 1) * cols].reshape(2 * cols, cols), weave).astype(jnp.bfloat16)
        out_ref[:cols, k * cols:(k + 1) * cols] = block[:, :cols]
        out_ref[cols:, k * cols:(k + 1) * cols] = block[:, cols:]
    part = both_send.at[:, pl.ds(0, width - channels)]
    pltpu.make_async_copy(part, part, send_sem.at[0]).wait()
    part = y_in.at[pl.ds(0, width - channels)]
    pltpu.make_async_copy(part, part, send_sem.at[1]).wait()


def body(activations, short_filters, long_filters, skip_gain):
    tokens, width = activations.shape[1:]
    segs, seqs = lax.axis_size("segment"), lax.axis_size("seq")
    mine = width // (segs * seqs)
    cols = COLS
    per = tokens // cols
    rows = 2 * per * seqs
    scale = 1.0 / (rows * cols * math.sqrt(rows * cols // 2))
    tabs = tables(rows, cols)
    kept = tabs[4].shape[1]
    vm = pl.BlockSpec(memory_space=pltpu.VMEM)
    far = pl.BlockSpec(memory_space=pl.ANY)
    grid = (2, mine, seqs, per, cols)
    chunks = (width, per, cols)
    vmem = lambda *shape: pltpu.VMEM(shape, jnp.bfloat16)
    like = lambda a: pltpu.VMEM(a.shape, a.dtype)
    x, f = activations[0], long_filters[0]
    dma = pltpu.SemaphoreType.DMA
    out = pl.pallas_call(
        functools.partial(kernel, scale, kept),
        out_shape=pltpu.VMEM((tokens, width), jnp.bfloat16),
        in_specs=[far] * 9,
        out_specs=vm,
        scratch_shapes=[
            like(x), like(f), like(short_filters), like(skip_gain), *[like(t) for t in tabs],
            vmem(2, *chunks), vmem(2, *grid), vmem(*grid), vmem(*chunks),
            pltpu.VMEM((2, mine, kept, 2 * cols), jnp.float32), vmem(2, mine, 2 * cols, cols),
            dma((9,)), dma((2,)), dma((3,)), dma,
        ],
        compiler_params=pltpu.CompilerParams(
            vmem_limit_bytes=54900 * 1024, has_side_effects=True, collective_id=0
        ),
    )(x, f, short_filters, skip_gain, *tabs)
    return out[None]


def solution(mesh):
    return jax.shard_map(
        body,
        mesh=mesh,
        in_specs=(P("segment", "seq", None), P(), P("segment", "seq", None), P()),
        out_specs=P("segment", "seq", None),
        check_vma=False,
    )
```
